512 devices in a mesh: dp: 16 (over z, core), ctx: 32 (over y, x).
Axes of the slice: x: 4, y: 8, z: 8, core: 2. Of those that a mesh axis runs over, the one named last changes fastest.
Arguments:
- query_in: bfloat16 [16, 8192, 1280], P('dp', 'ctx'), may hold values from -150 to 150
- key_in: bfloat16 [16, 8192, 1280], P('dp', 'ctx'), may hold values from -16 to 16
- value_in: bfloat16 [16, 8192, 1280], P('dp', 'ctx'), may hold values from -6 to 6
- grad_out: bfloat16 [16, 8192, 1280], P('dp', 'ctx'), may hold values from -6 to 6
- key_blocks: int32 [10, 32, 6], P(None, 'ctx'), may hold values from 0 to 63, as said below
- sink_logits: float32 [10], replicated, may hold values from 3 to 8
Outputs:
- grad_query: bfloat16 [16, 8192, 1280], P('dp', 'ctx')
- grad_key: bfloat16 [16, 8192, 1280], P('dp', 'ctx')
- grad_value: bfloat16 [16, 8192, 1280], P('dp', 'ctx')
- grad_sink: float32 [10], replicated
The draws below stay inside these ranges and needn't reach their ends.
Inputs may be any that keep to these rules, and one draw needn't show every extreme that they name: `key_blocks`: block b holds tokens 128 b to 128 b + 127. The 6 entries of one head and segment are distinct, and none falls in the aligned group of 256 tokens that holds the segment. Counting all heads, entries and segments of one aligned group of 256 tokens, at most 2 entries fall in any one other aligned group of 256 tokens, and every group reaches 2 with some other group in every draw.
All inputs are finite; a program needn't handle non-finite values.
Results may differ from the reference program's by a relative error of at most 0.012.
Values may be sent and summed in bfloat16 or wider, within the bound.
A program may use at most 64 MiB of HBM per device.

```python
import math
import jax
import jax.numpy as jnp
from jax import lax

TOK_DEV = 256
H = 10
HD = 128
BLOCK = 128
SEG_BLOCKS = 2
KR = 6
B = 16
L = 8192
NB = 64
NSEG = 32
SEG_DEV = 1
CAP = 2


def paired_fields(key):
    base_key = jax.random.fold_in(key, 7)
    key_one, key_two = jax.random.split(base_key, 2)
    shape_all = (B, L, H * HD)
    key_field = jnp.clip(jax.random.normal(key_one, shape_all, jnp.float32), -5.0, 5.0)
    query_field = jnp.clip(jax.random.normal(key_two, shape_all, jnp.float32), -5.0, 5.0)
    return (query_field, key_field)


def draw_query_in(key, part):
    return paired_fields(key)[0].astype(jnp.bfloat16)


def draw_key_in(key, part):
    return paired_fields(key)[1].astype(jnp.bfloat16)


def draw_key_blocks(key, part):
    groups = NSEG // SEG_DEV
    per_group = TOK_DEV // BLOCK
    requests = SEG_DEV * H * KR
    key_one, key_two = jax.random.split(jax.random.fold_in(key, 3))
    sources = jnp.arange(groups, dtype=jnp.int32)
    offsets = jnp.arange(groups - 1, dtype=jnp.int32)
    owners_all = (sources[:, None] + 1 + offsets[None, :]) % groups
    ranking = (jax.random.randint(key_one, (groups, groups - 1), 0, groups, dtype=jnp.int32) + owners_all) * groups + offsets[None, :]
    visit_order = jnp.argsort(ranking, axis=1, stable=True).astype(jnp.int32)
    picks = jnp.arange(requests, dtype=jnp.int32) // CAP
    owners = (sources[:, None] + 1 + visit_order[:, picks]) % groups
    within = jax.random.randint(key_two, (groups, requests), 0, per_group, dtype=jnp.int32)
    blocks = owners * per_group + within
    return jnp.transpose(blocks.reshape(groups, KR, H, SEG_DEV), (2, 0, 3, 1)).reshape(H, NSEG, KR)


def block_scale(rng, shape, pieces, smallest, largest):
    gain, own = 1.0, jax.random.fold_in(rng, 6)
    for dim, blocks in pieces:
        heights = jnp.exp(jax.random.uniform(jax.random.fold_in(own, dim), (blocks,), jnp.float32, smallest / len(pieces), largest / len(pieces)))
        gain = gain * jnp.repeat(heights, shape[dim] // blocks).reshape([-1 if axis == dim else 1 for axis in range(len(shape))])
    return gain


def gaussian(stream_key, extent, spread, limit, cuts=(), held_as=jnp.bfloat16):
    entries = jax.random.normal(stream_key, extent, jnp.float32) * spread
    if len(cuts) > 0:
        entries = block_scale(stream_key, extent, cuts, -0.22, 0.18) * entries
    return jnp.clip(entries, min=-limit, max=limit).astype(held_as)


def setup_inputs(seed: int = 0) -> dict:
    arg_keys = jax.random.split(jax.random.key(seed), 7)
    return {
        "query_in": draw_query_in(jax.random.fold_in(arg_keys[6], 71), 0),
        "key_in": draw_key_in(jax.random.fold_in(arg_keys[6], 71), 0),
        "value_in": gaussian(arg_keys[2], (B, L, H * HD), 1.0, 6.0, ((0, 16), (1, 32))),
        "grad_out": gaussian(arg_keys[3], (B, L, H * HD), 1.0, 6.0, ((0, 16), (1, 32))),
        "key_blocks": draw_key_blocks(jax.random.fold_in(arg_keys[6], 71), 0),
        "sink_logits": jnp.clip(jax.random.uniform(arg_keys[5], (H,), jnp.float32, 3.0, 8.0), 3.0, 8.0),
    }


def head_pass(inputs):
    query_h, key_h, value_h, grad_h, block_rows, sink_h = inputs
    seg_len = SEG_BLOCKS * BLOCK
    scaling = 1.0 / math.sqrt(HD)
    block_ids = block_rows.astype(jnp.int32)

    def keyed(field):
        own_part = field.reshape(NSEG, seg_len, HD)
        listed = field.reshape(NB, BLOCK, HD)[block_ids].reshape(NSEG, KR * BLOCK, HD)
        return jnp.concatenate([own_part, listed], axis=1).astype(jnp.float32)
    key_all = keyed(key_h)
    value_all = keyed(value_h)
    query_f = query_h.reshape(NSEG, seg_len, HD).astype(jnp.float32)
    grad_f = grad_h.reshape(NSEG, seg_len, HD).astype(jnp.float32)
    scores = jnp.einsum('sqd,skd->sqk', query_f, key_all) * scaling
    row_top = jnp.maximum(lax.optimization_barrier(jnp.max(scores, axis=-1)), sink_h)
    row_total = jnp.exp(sink_h - row_top) + lax.optimization_barrier(jnp.sum(jnp.exp(scores - row_top[..., None]), axis=-1))
    log_norm = row_top + jnp.log(row_total)
    weights = jnp.exp(scores - log_norm[..., None])
    prob_f = lax.optimization_barrier(weights.astype(jnp.bfloat16)).astype(jnp.float32)
    attended = jnp.einsum('sqk,skd->sqd', prob_f, value_all).astype(jnp.bfloat16)
    attended_f = lax.optimization_barrier(attended).astype(jnp.float32)
    row_delta = lax.optimization_barrier(jnp.sum(grad_f * attended_f, axis=-1))
    dprobs = jnp.einsum('sqd,skd->sqk', grad_f, value_all)
    dscores = weights * (dprobs - row_delta[..., None])
    dscores = lax.optimization_barrier(dscores.astype(jnp.bfloat16)).astype(jnp.float32)
    grad_q = (jnp.einsum('sqk,skd->sqd', dscores, key_all) * scaling).astype(jnp.bfloat16).reshape(L, HD)
    key_terms = jnp.einsum('sqk,sqd->skd', dscores, query_f) * scaling
    value_terms = jnp.einsum('sqk,sqd->skd', prob_f, grad_f)

    def settle(all_terms):
        own_part = all_terms[:, :seg_len].reshape(L, HD)
        listed = lax.optimization_barrier(all_terms[:, seg_len:].astype(jnp.bfloat16)).astype(jnp.float32)
        listed = listed.reshape(NSEG * KR, BLOCK, HD)
        summed = jnp.zeros((NB, BLOCK, HD), jnp.float32).at[block_ids.reshape(-1)].add(listed)
        return (own_part + summed.reshape(L, HD)).astype(jnp.bfloat16)
    sink_part = -jnp.sum(jnp.exp(sink_h - log_norm) * row_delta)
    return (grad_q, settle(key_terms), settle(value_terms), sink_part)

def reference(query_in, key_in, value_in, grad_out, key_blocks, sink_logits):

    def split_heads(field):
        return jnp.transpose(field.reshape(L, H, HD), (1, 0, 2))

    def join_heads(field):
        return jnp.transpose(field, (1, 0, 2)).reshape(L, H * HD)

    def sequence_pass(inputs):
        query_s, key_s, value_s, grad_s = inputs
        grad_q, grad_k, grad_v, sink_parts = lax.map(head_pass, (split_heads(query_s), split_heads(key_s), split_heads(value_s), split_heads(grad_s), key_blocks, sink_logits))
        return (join_heads(grad_q), join_heads(grad_k), join_heads(grad_v), sink_parts)
    grad_query, grad_key, grad_value, sink_all = lax.map(sequence_pass, (query_in, key_in, value_in, grad_out))
    return (grad_query, grad_key, grad_value, lax.optimization_barrier(jnp.sum(sink_all, axis=0)))
```

```python
from functools import partial
import math

import jax
import jax.numpy as jnp
from jax import lax
from jax.experimental import pallas as pl
from jax.experimental.pallas import tpu as pltpu
from jax.sharding import PartitionSpec as P

BLOCK = 128
SEG = 256
HD = 128
HEADS = 10
NSEG = 32
HALF = NSEG // 2
LISTED = 6
ROWS = NSEG * SEG
HROWS = HALF * SEG
CHUNKS = 4
LOG2E = math.log2(math.e)
SCALE = 1.0 / math.sqrt(HD)
MESH = pl.DeviceIdType.MESH


def div(a, b):
    return lax.div(a, jnp.int32(b))


def rem(a, b):
    return lax.rem(a, jnp.int32(b))


def home_ctx(core, head):
    pair = core * HEADS + head
    j = div(pair, 5)
    r = rem(pair, 5)
    odd = div(r, 3)
    x = rem(r + j + 8 + odd * (r - 6), 4)
    return 4 * (2 * j + odd) + x


def my_pair(ctx):
    y = div(ctx, 4)
    j = div(y, 2)
    odd = rem(y, 2)
    u = rem(rem(ctx, 4) + 4 - j, 4)
    is_home = ((1 - odd) * div(u, 3) + odd * rem(u, 2)) == 0
    r = (1 - odd) * u + odd * (3 + div(u, 2))
    pair = 5 * j + r
    return is_home, div(pair, HEADS), rem(pair, HEADS)


class Place:
    def __init__(self):
        dp = lax.axis_index("dp")
        self.ctx = lax.axis_index("ctx")
        self.core = rem(dp, 2)
        self.plane = dp - self.core
        self.is_home, self.pair_core, self.pair_head = my_pair(self.ctx)
        self.target_core = 1 - div(self.ctx, HALF)
        self.half = 1 - self.core
        self.sibling = (self.plane + 1 - self.core, self.ctx)

    def home(self, head):
        return (self.plane + self.target_core, home_ctx(self.core, head))

    def owner(self, j):
        return (self.plane + self.pair_core, self.half * HALF + j)


def greet(place):
    barrier = pltpu.get_barrier_semaphore()

    @pl.loop(0, HEADS)
    def _(i):
        pl.semaphore_signal(barrier, inc=1, device_id=place.home(i), device_id_type=MESH)

    @pl.when(place.is_home)
    def _():
        @pl.loop(0, HALF)
        def _(j):
            pl.semaphore_signal(barrier, inc=1, device_id=place.owner(j), device_id_type=MESH)

        pl.semaphore_signal(barrier, inc=1, device_id=place.sibling, device_id_type=MESH)

    pl.semaphore_wait(barrier, HEADS + place.is_home.astype(jnp.int32) * (HALF + 1))


def columns(head):
    return pl.ds(pl.multiple_of(head * HD, HD), HD)


def rows_of(start, size):
    return pl.ds(pl.multiple_of(start, size), size)


def collect_kernel(
    q_in, k_in, v_in, g_in, lists_in, q_out, g_out, k_out, v_out, lists_out,
    send_sem, recv_sem, list_send, list_recv, swap_send, swap_recv,
):
    place = Place()
    greet(place)
    seg_rows = rows_of(place.ctx * SEG, SEG)
    loc_rows = rows_of(rem(place.ctx, HALF) * SEG, SEG)

    def remote(src, dst, ssem, rsem, target):
        return pltpu.make_async_remote_copy(
            src_ref=src, dst_ref=dst, send_sem=ssem, recv_sem=rsem,
            device_id=target, device_id_type=MESH,
        )

    @pl.loop(0, HEADS)
    def _(i):
        head = rem(place.ctx + i, HEADS)
        cols = columns(head)
        target = place.home(head)
        remote(k_in.at[0, :, cols], k_out.at[seg_rows], send_sem.at[0], recv_sem.at[0], target).start()
        remote(v_in.at[0, :, cols], v_out.at[seg_rows], send_sem.at[1], recv_sem.at[1], target).start()

    @pl.loop(0, HEADS)
    def _(i):
        head = rem(place.ctx + i, HEADS)
        cols = columns(head)
        target = place.home(head)
        remote(lists_in.at[head], lists_out.at[rem(place.ctx, HALF)], list_send, list_recv, target).start()
        remote(q_in.at[0, :, cols], q_out.at[loc_rows], send_sem.at[2], recv_sem.at[2], target).start()
        remote(g_in.at[0, :, cols], g_out.at[loc_rows], send_sem.at[3], recv_sem.at[3], target).start()

    @pl.when(place.is_home)
    def _():
        mine = rows_of(place.half * HROWS, HROWS)
        other = rows_of(place.core * HROWS, HROWS)
        for t, ref in enumerate((k_out, v_out)):
            part = ref.at[mine]
            remote(part, part, send_sem.at[t], recv_sem.at[t], place.sibling).wait_recv()
            remote(part, part, swap_send.at[t], swap_recv.at[t], place.sibling).start()
        remote(lists_out, lists_out, list_send, list_recv, place.sibling).wait_recv()
        remote(q_out, q_out, send_sem.at[2], recv_sem.at[2], place.sibling).wait_recv()
        remote(g_out, g_out, send_sem.at[3], recv_sem.at[3], place.sibling).wait_recv()
        for t, ref in enumerate((k_out, v_out)):
            remote(ref.at[mine], ref.at[other], swap_send.at[t], swap_recv.at[t], place.sibling).wait()

    remote(lists_in, lists_in, list_send, list_recv, place.sibling).wait_send()
    for t, ref in enumerate((k_in, v_in, q_in, g_in)):
        remote(ref, ref, send_sem.at[t], recv_sem.at[t], place.sibling).wait_send()


def fold(x, op):
    return op(x.reshape(x.shape[0] // 8, 8, x.shape[1]), axis=0)


NT = (((1,), (1,)), ((), ()))
TN = (((0,), (0,)), ((), ()))


def attend_kernel(
    lists, sinks, q_ref, g_ref, k_ref, v_ref,
    dq_ref, own_k, own_v, far_k, far_v, sink_out,
    e_ref, p_ref, acc_k, acc_v,
):
    sink_out[...] = jnp.zeros_like(sink_out)
    place = Place()

    @pl.when(place.is_home)
    def _():
        half = place.half
        sink2 = sinks[place.pair_head] * LOG2E
        acc_k[...] = jnp.zeros_like(acc_k)
        acc_v[...] = jnp.zeros_like(acc_v)

        @pl.loop(0, HALF)
        def _(j):
            q = q_ref[rows_of(j * SEG, SEG), :]
            g = g_ref[rows_of(j * SEG, SEG), :]
            spans = [(rows_of((half * HALF + j) * SEG, SEG), 0, SEG)]
            for m in range(LISTED):
                spans.append((rows_of(lists[j, 0, m] * BLOCK, BLOCK), SEG + m * BLOCK, BLOCK))
            top8 = None
            for src, at, size in spans:
                s = lax.dot_general(k_ref[src, :], q, NT, preferred_element_type=jnp.float32)
                e_ref[at:at + size, :] = s
                high = fold(s, jnp.max)
                top8 = high if top8 is None else jnp.maximum(top8, high)
            factor = SCALE * LOG2E
            top = jnp.maximum(jnp.max(top8, axis=0, keepdims=True) * factor, sink2)
            sum8 = jnp.zeros((8, SEG), jnp.float32)
            dot8 = jnp.zeros((8, SEG), jnp.float32)
            for src, at, size in spans:
                dp = lax.dot_general(v_ref[src, :], g, NT, preferred_element_type=jnp.float32)
                e = jnp.exp2(e_ref[at:at + size, :] * factor - top)
                e_ref[at:at + size, :] = e
                p_ref[at:at + size, :] = dp
                sum8 = sum8 + fold(e, jnp.sum)
                dot8 = dot8 + fold(e * dp, jnp.sum)
            sink_e = jnp.exp2(sink2 - top)
            total = sink_e + jnp.sum(sum8, axis=0, keepdims=True)
            inv = 1.0 / total
            delta = jnp.sum(dot8, axis=0, keepdims=True) * inv
            sink_out[...] = sink_out[...] - sink_e * inv * delta
            dq_t = jnp.zeros((HD, SEG), jnp.float32)
            for src, at, size in spans:
                w = e_ref[at:at + size, :] * inv
                ds = (w * (p_ref[at:at + size, :] - delta)).astype(jnp.bfloat16)
                w = w.astype(jnp.bfloat16)
                acc_v[src, :] += jnp.dot(w, g, preferred_element_type=jnp.float32)
                acc_k[src, :] += jnp.dot(ds, q, preferred_element_type=jnp.float32)
                dq_t = dq_t + lax.dot_general(k_ref[src, :], ds, TN, preferred_element_type=jnp.float32)
            dq_ref[rows_of(j * SEG, SEG), :] = (dq_t * SCALE).T.astype(jnp.bfloat16)

        mine = rows_of(half * HROWS, HROWS)
        other = rows_of((1 - half) * HROWS, HROWS)
        own_k[...] = acc_k[mine, :] * SCALE
        own_v[...] = acc_v[mine, :]
        far_k[...] = (acc_k[other, :] * SCALE).astype(jnp.bfloat16)
        far_v[...] = acc_v[other, :].astype(jnp.bfloat16)


def return_kernel(
    dq, own_k, own_v, far_k, far_v, gq, gk, gv, near_k, near_v, fin_k, fin_v,
    send_sem, recv_sem, swap_send, swap_recv,
):
    place = Place()
    greet(place)

    def remote(src, dst, ssem, rsem, target):
        return pltpu.make_async_remote_copy(
            src_ref=src, dst_ref=dst, send_sem=ssem, recv_sem=rsem,
            device_id=target, device_id_type=MESH,
        )

    step = HROWS // CHUNKS
    pairs = ((far_k, near_k, own_k, fin_k, gk), (far_v, near_v, own_v, fin_v, gv))

    @pl.when(place.is_home)
    def _():
        cols = columns(place.pair_head)
        for c in range(CHUNKS):
            part = pl.ds(c * step, step)
            for t, (far, near, _, _, _) in enumerate(pairs):
                remote(far.at[part], near.at[part], swap_send.at[t, c], swap_recv.at[t, c], place.sibling).start()

        @pl.loop(0, HALF)
        def _(i):
            j = rem(place.ctx + i, HALF)
            rows = rows_of(j * SEG, SEG)
            remote(dq.at[rows], gq.at[0, :, cols], send_sem.at[2], recv_sem.at[2], place.owner(j)).start()

        for c in range(CHUNKS):
            part = pl.ds(c * step, step)
            for t, (far, near, own, fin, out) in enumerate(pairs):
                remote(far.at[part], near.at[part], swap_send.at[t, c], swap_recv.at[t, c], place.sibling).wait()
                fin[part, :] = (own[part, :] + near[part, :].astype(jnp.float32)).astype(jnp.bfloat16)

                @pl.loop(0, HALF // CHUNKS)
                def _(i):
                    j = c * (HALF // CHUNKS) + i
                    rows = rows_of(j * SEG, SEG)
                    remote(fin.at[rows], out.at[0, :, cols], send_sem.at[t], recv_sem.at[t], place.owner(j)).start()

        remote(fin_k, fin_k, send_sem.at[0], recv_sem.at[0], place.sibling).wait_send()
        remote(fin_v, fin_v, send_sem.at[1], recv_sem.at[1], place.sibling).wait_send()
        remote(dq, dq, send_sem.at[2], recv_sem.at[2], place.sibling).wait_send()

    for t, ref in enumerate((gk, gv, gq)):
        remote(ref, ref, send_sem.at[t], recv_sem.at[t], place.sibling).wait_recv()


def body(query_in, key_in, value_in, grad_out, key_blocks, sink_logits):
    bf16, f32 = jnp.bfloat16, jnp.float32
    any_spec = pl.BlockSpec(memory_space=pl.ANY)
    vmem_spec = pl.BlockSpec(memory_space=pltpu.VMEM)
    smem_spec = pl.BlockSpec(memory_space=pltpu.SMEM)
    dma = pltpu.SemaphoreType.DMA
    shape = jax.ShapeDtypeStruct
    lists = jnp.pad(key_blocks, ((0, 0), (0, 0), (0, BLOCK - LISTED)))
    q_all, g_all, k_all, v_all, lists_all = pl.pallas_call(
        collect_kernel,
        out_shape=(
            shape((HROWS, HD), bf16), shape((HROWS, HD), bf16),
            shape((ROWS, HD), bf16), shape((ROWS, HD), bf16),
            shape((HALF, 1, BLOCK), jnp.int32),
        ),
        in_specs=[any_spec] * 5,
        out_specs=(any_spec,) * 5,
        scratch_shapes=[dma((4,)), dma((4,)), dma, dma, dma((2,)), dma((2,))],
        compiler_params=pltpu.CompilerParams(collective_id=0, has_side_effects=True),
        name="collect",
    )(query_in, key_in, value_in, grad_out, lists)

    place = Place()
    dq, own_k, own_v, far_k, far_v, sink_part = pl.pallas_call(
        attend_kernel,
        out_shape=(
            shape((HROWS, HD), bf16), shape((HROWS, HD), f32), shape((HROWS, HD), f32),
            shape((HROWS, HD), bf16), shape((HROWS, HD), bf16), shape((1, SEG), f32),
        ),
        in_specs=[smem_spec] * 2 + [vmem_spec] * 4,
        out_specs=(vmem_spec,) * 6,
        scratch_shapes=[
            pltpu.VMEM((SEG + LISTED * BLOCK, SEG), f32), pltpu.VMEM((SEG + LISTED * BLOCK, SEG), f32),
            pltpu.VMEM((ROWS, HD), f32), pltpu.VMEM((ROWS, HD), f32),
        ],
        compiler_params=pltpu.CompilerParams(vmem_limit_bytes=50 * 2**20),
        name="attend",
    )(lists_all, sink_logits, q_all, g_all, k_all, v_all)

    sink_vec = jnp.where(
        (jnp.arange(HEADS) == place.pair_head) & place.is_home, jnp.sum(sink_part), 0.0
    )
    grad_sink = lax.psum(sink_vec, ("dp", "ctx"))

    tok = query_in.shape
    gq, gk, gv = pl.pallas_call(
        return_kernel,
        out_shape=(shape(tok, bf16),) * 3,
        in_specs=[any_spec, vmem_spec, vmem_spec, any_spec, any_spec],
        out_specs=(any_spec,) * 3,
        scratch_shapes=[
            pltpu.VMEM((HROWS, HD), bf16), pltpu.VMEM((HROWS, HD), bf16),
            pltpu.VMEM((HROWS, HD), bf16), pltpu.VMEM((HROWS, HD), bf16),
            dma((3,)), dma((3,)), dma((2, CHUNKS)), dma((2, CHUNKS)),
        ],
        compiler_params=pltpu.CompilerParams(
            collective_id=1, has_side_effects=True, vmem_limit_bytes=40 * 2**20
        ),
        name="give_back",
    )(dq, own_k, own_v, far_k, far_v)
    return (gq, gk, gv, grad_sink)


def solution(mesh):
    placed = (
        P("dp", "ctx", None),
        P("dp", "ctx", None),
        P("dp", "ctx", None),
        P("dp", "ctx", None),
        P(None, "ctx", None),
        P(),
    )
    return jax.shard_map(
        body,
        mesh=mesh,
        in_specs=placed,
        out_specs=(P("dp", "ctx", None), P("dp", "ctx", None), P("dp", "ctx", None), P()),
        check_vma=False,
    )
```

```python
import math

import jax
import jax.numpy as jnp
from jax import lax
from jax.experimental import pallas as pl
from jax.experimental.pallas import tpu as pltpu
from jax.sharding import PartitionSpec as P

BLOCK = 128
SEG = 256
HD = 128
HEADS = 10
NSEG = 32
HALF = NSEG // 2
LISTED = 6
KEYS = SEG + LISTED * BLOCK
SLOT = 8
EMPTY = 6
CHUNKS = 4
EARLY = 10
PLANES = 8
LOG2E = math.log2(math.e)
SCALE = 1.0 / math.sqrt(HD)
MESH = pl.DeviceIdType.MESH
F32 = jnp.float32
BF16 = jnp.bfloat16
NT = (((1,), (1,)), ((), ()))
TN = (((0,), (0,)), ((), ()))


def div(a, b):
    return lax.div(a, jnp.int32(b))


def rem(a, b):
    return lax.rem(a, jnp.int32(b))


def home_ctx(core, head):
    j = 2 * div(head, 5) + core
    r = rem(head, 5)
    odd = div(r, 3)
    x = rem(r + j + 8 + odd * (r - 6), 4)
    return 4 * (2 * j + odd) + x


def my_pair(ctx):
    y = div(ctx, 4)
    j = div(y, 2)
    odd = rem(y, 2)
    u = rem(rem(ctx, 4) + 4 - j, 4)
    is_home = ((1 - odd) * div(u, 3) + odd * rem(u, 2)) == 0
    r = (1 - odd) * u + odd * (3 + div(u, 2))
    return is_home, rem(j, 2), 5 * div(j, 2) + r


def half_of(s):
    return rem(div(s, 8), 2)


def local_of(s):
    return 8 * div(s, HALF) + rem(s, 8)


def segment(half, j):
    return HALF * div(j, 8) + 8 * half + rem(j, 8)


def is_spare(y, x):
    u = rem(x + 4 - div(y, 2), 4)
    odd = rem(y, 2)
    return ((1 - odd) * div(u, 3) + odd * rem(u, 2)) == 1


def turn(head, j):
    m = rem(div(8 * head, 5) + HALF - j, HALF)
    return 2 * rem(m, HALF // 2) + div(m, HALF // 2)


def taken(head, n):
    m = div(n, 2) + (HALF // 2) * rem(n, 2)
    return rem(div(8 * head, 5) + HALF - m, HALF)


class Place:
    def __init__(self):
        dp = lax.axis_index("dp")
        self.ctx = lax.axis_index("ctx")
        self.core = rem(dp, 2)
        self.plane = dp - self.core
        self.is_home, self.pair_core, self.pair_head = my_pair(self.ctx)
        self.target_core = 1 - half_of(self.ctx)
        self.half = 1 - self.core
        self.local = local_of(self.ctx)
        self.first = rem(div(5 * self.local + 7, 8), HEADS)
        self.sibling = (self.plane + 1 - self.core, self.ctx)
        self.y = div(self.ctx, 4)
        self.x = rem(self.ctx, 4)
        self.odd = rem(self.y, 2)
        self.spares = 1 + self.odd
        self.homes = 3 - self.odd
        self.row_head = 5 * div(self.y, 4) + 3 * self.odd
        self.row_core = rem(div(self.y, 2), 2)
        self.inside = (self.row_core == self.half).astype(jnp.int32)
        twin = home_ctx(1 - self.pair_core, self.pair_head)
        self.twins = ((self.plane, twin), (self.plane + 1, twin))

    def home(self, head):
        return (self.plane + self.target_core, home_ctx(self.core, head))

    def sent_to(self, i):
        return rem(self.first + div(i, 2) + (HEADS // 2) * rem(i, 2), HEADS)

    def owner(self, j):
        return (self.plane + self.pair_core, segment(self.half, j))

    def row_home(self, i):
        head = self.row_head + i
        return head, (self.plane + self.core, home_ctx(self.row_core, head))

    def relayed(self, j):
        x = rem(j, 4)
        device = (self.plane + self.core, 4 * self.y + x)
        return is_spare(self.y, x) & (div(segment(self.half, j), 4) != self.y), device

    def other_plane(self, i):
        return (rem(self.plane + self.core + 2 * i, 2 * PLANES), self.ctx)


def greet(place):
    barrier = pltpu.get_barrier_semaphore()

    def signal(device):
        pl.semaphore_signal(barrier, inc=1, device_id=device, device_id_type=MESH)

    @pl.loop(0, HEADS)
    def _(i):
        signal(place.home(i))

    @pl.loop(0, 4)
    def _(i):
        y = 4 * div(i, 2) + 2 * place.core + rem(i, 2)

        @pl.when(is_spare(y, place.x) & (y != place.y))
        def _():
            signal((place.plane + place.target_core, 4 * y + place.x))

    @pl.when(jnp.logical_not(place.is_home))
    def _():
        @pl.loop(0, place.homes)
        def _(i):
            signal(place.row_home(i)[1])

    @pl.when(place.is_home)
    def _():
        @pl.loop(0, HALF)
        def _(j):
            signal(place.owner(j))

        signal(place.sibling)
        for twin in place.twins:
            signal(twin)

        @pl.loop(1, PLANES)
        def _(i):
            signal(place.other_plane(i))

    home = place.is_home.astype(jnp.int32)
    peers = HALF + 1 + 2 + PLANES - 1 + place.spares
    pl.semaphore_wait(barrier, HEADS + home * peers + (1 - home) * (4 - place.inside))


def remote(src, dst, ssem, rsem, target):
    return pltpu.make_async_remote_copy(
        src_ref=src, dst_ref=dst, send_sem=ssem, recv_sem=rsem,
        device_id=target, device_id_type=MESH,
    )


def columns(head):
    return pl.ds(pl.multiple_of(head * HD, HD), HD)


def rows_of(start, size):
    return pl.ds(pl.multiple_of(start, size), size)


def fold(x, op):
    return op(x.reshape(x.shape[0] // 8, 8, x.shape[1]), axis=0)


def highest(x):
    part = x[0:8]
    for i in range(8, x.shape[0], 8):
        part = jnp.maximum(part, x[i:i + 8])
    row = part[0:1]
    for i in range(1, 8):
        row = jnp.maximum(row, part[i:i + 1])
    return row


def write_tables(lists, table):
    row = lists[0]
    for j in range(1, HALF):
        row = row + lists[j]
    row = row - 1
    shape = (BLOCK, BLOCK)
    wide = jnp.broadcast_to(row, shape)
    tall = wide.T
    entry = lax.broadcasted_iota(jnp.int32, shape, 0)
    lane = lax.broadcasted_iota(jnp.int32, shape, 1)
    before = highest(jnp.where((tall == wide) & (entry < lane), entry, -1))
    last = highest(jnp.where(tall == lane, entry, -1))
    place = jnp.maximum(row, 0)
    block = lax.bitwise_and(place, 1)
    s = lax.shift_right_logical(place, 1)
    half = lax.bitwise_and(lax.shift_right_logical(s, 3), 1)
    local = 8 * lax.shift_right_logical(s, 4) + lax.bitwise_and(s, 7)
    table[0:1, :] = 4 * (half * HALF + local) + block
    table[1:2, :] = jnp.where(before < 0, EMPTY, before)
    table[2:3, :] = jnp.where(last < 0, EMPTY, last)


def fused_kernel(
    q_in, k_in, v_in, g_in, lists_in, sinks, gq, gk, gv, sink_out,
    kv, qg, lists, table, entries, dq, term_k, term_v, own_k, own_v, far, near, fin, e_ref, p_ref,
    sink_sum, sink_a, sink_b, sink_c,
    list_send, list_recv, kv_send, kv_recv, swap_send, swap_recv, qg_send, qg_recv, dq_send, fin_send,
    relay_dq, relay_kv, relay_dq_recv, relay_kv_recv, relay_send,
    out_recv, far_send, far_recv, a_send, a_recv, b_send, b_recv, c_send, c_recv, table_sem,
):
    place = Place()
    greet(place)
    head_of = place.pair_head

    @pl.loop(0, HEADS)
    def _(i):
        head = place.sent_to(i)
        target = place.home(head)
        remote(lists_in.at[head], lists.at[place.local], list_send, list_recv, target).start()

    @pl.loop(0, HEADS)
    def _(i):
        head = place.sent_to(i)
        cols = columns(head)
        target = place.home(head)
        at = 4 * ((1 - place.target_core) * HALF + place.local)
        sem = kv_recv.at[place.local]
        remote(k_in.at[:, :, cols], kv.at[pl.ds(at, 2)], kv_send.at[0], sem, target).start()
        remote(v_in.at[:, :, cols], kv.at[pl.ds(at + 2, 2)], kv_send.at[1], sem, target).start()

    def pass_on(start, stop):
        @pl.loop(start, stop)
        def _(n):
            j = taken(head_of, n)
            part = kv.at[pl.ds(4 * (place.half * HALF + j), 4)]
            remote(part, part, kv_send.at[0], kv_recv.at[j], place.sibling).wait_recv()
            remote(part, part, swap_send, swap_recv, place.sibling).start()

    @pl.when(place.is_home)
    def _():
        remote(lists, lists, list_send, list_recv, place.sibling).wait_recv()
        write_tables(lists, table)
        down = pltpu.make_async_copy(table, entries, table_sem)
        down.start()
        term_k[EMPTY] = jnp.zeros((BLOCK, HD), F32)
        term_v[EMPTY] = jnp.zeros((BLOCK, HD), F32)
        sink_sum[...] = jnp.zeros_like(sink_sum)
        down.wait()

        pass_on(0, EARLY)

    for t, ref in enumerate((k_in, v_in)):
        remote(ref, ref, kv_send.at[t], kv_recv.at[0], place.sibling).wait_send()

    @pl.loop(0, HEADS)
    def _(i):
        head = place.sent_to(i)
        cols = columns(head)
        target = place.home(head)
        at = place.local * (2 * SEG)
        sem = qg_recv.at[place.local]
        remote(q_in.at[0, :, cols], qg.at[rows_of(at, SEG)], qg_send.at[0], sem, target).start()
        remote(g_in.at[0, :, cols], qg.at[rows_of(at + SEG, SEG)], qg_send.at[1], sem, target).start()

    @pl.when(place.is_home)
    def _():
        cols = columns(head_of)
        pass_on(EARLY, HALF)
        mine = kv.at[pl.ds(place.half * (4 * HALF), 4 * HALF)]
        other = kv.at[pl.ds(place.core * (4 * HALF), 4 * HALF)]
        remote(mine, other, swap_send, swap_recv, place.sibling).wait()
        sink2 = sinks[head_of] * LOG2E

        @pl.loop(0, HALF)
        def _(n):
            j = taken(head_of, n)
            part = qg.at[rows_of(j * (2 * SEG), 2 * SEG)]
            remote(part, part, qg_send.at[0], qg_recv.at[j], place.sibling).wait_recv()
            q = qg[rows_of(j * (2 * SEG), SEG), :]
            g = qg[rows_of(j * (2 * SEG) + SEG, SEG), :]
            spans = [(4 * (place.half * HALF + j), 0, SEG)]
            for m in range(LISTED):
                spans.append((entries[0, n * SLOT + m], SEG + m * BLOCK, BLOCK))

            def keyed(src, size):
                return kv[pl.ds(src, 2)].reshape(SEG, HD) if size == SEG else kv[src]

            top8 = None
            for src, at, size in spans:
                k = keyed(src, size)
                s = lax.dot_general(k, q, NT, preferred_element_type=F32)
                e_ref[at:at + size, :] = s
                high = fold(s, jnp.max)
                top8 = high if top8 is None else jnp.maximum(top8, high)
            factor = SCALE * LOG2E
            top = jnp.maximum(jnp.max(top8, axis=0, keepdims=True) * factor, sink2)
            sum8 = jnp.zeros((8, SEG), F32)
            dot8 = jnp.zeros((8, SEG), F32)
            for src, at, size in spans:
                v = keyed(src + 2, size)
                dp = lax.dot_general(v, g, NT, preferred_element_type=F32)
                e = jnp.exp2(e_ref[at:at + size, :] * factor - top)
                e_ref[at:at + size, :] = e
                p_ref[at:at + size, :] = dp
                sum8 = sum8 + fold(e, jnp.sum)
                dot8 = dot8 + fold(e * dp, jnp.sum)
            sink_e = jnp.exp2(sink2 - top)
            total = sink_e + jnp.sum(sum8, axis=0, keepdims=True)
            inv = 1.0 / total
            delta = jnp.sum(dot8, axis=0, keepdims=True) * inv
            sink_sum[...] = sink_sum[...] - sink_e * inv * delta
            dq_t = jnp.zeros((HD, SEG), F32)
            for m, (src, at, size) in enumerate(spans):
                w = e_ref[at:at + size, :] * inv
                ds = (w * (p_ref[at:at + size, :] - delta)).astype(BF16)
                w = w.astype(BF16)
                tv = jnp.dot(w, g, preferred_element_type=F32)
                tk = jnp.dot(ds, q, preferred_element_type=F32)
                if m == 0:
                    own_k[rows_of(n * SEG, SEG), :] = tk
                    own_v[rows_of(n * SEG, SEG), :] = tv
                else:
                    slot = n * SLOT + m - 1
                    before = entries[1, slot]
                    term_k[slot] = tk + term_k[before]
                    term_v[slot] = tv + term_v[before]
                k = keyed(src, size)
                dq_t = dq_t + lax.dot_general(k, ds, TN, preferred_element_type=F32)
            rows = rows_of(n * SEG, SEG)
            dq[rows, :] = (dq_t * SCALE).T.astype(BF16)
            by_relay, relay = place.relayed(j)
            slot = (head_of - place.row_head) * 4 + div(j, 4)

            @pl.when(by_relay)
            def _():
                to = relay_dq.at[rows_of(slot * SEG, SEG)]
                remote(dq.at[rows], to, dq_send, relay_dq_recv.at[slot], relay).start()

            @pl.when(jnp.logical_not(by_relay))
            def _():
                remote(dq.at[rows], gq.at[0, :, cols], dq_send, out_recv.at[0], place.owner(j)).start()

        step = HALF // CHUNKS
        for c in range(CHUNKS):
            @pl.loop(0, step)
            def _(i):
                n = c * step + i
                j = taken(head_of, n)
                for b in range(2):
                    last = entries[2, 2 * segment(place.core, j) + b]
                    at = n * (2 * SEG) + b * BLOCK
                    far[rows_of(at, BLOCK), :] = (term_k[last] * SCALE).astype(BF16)
                    far[rows_of(at + SEG, BLOCK), :] = term_v[last].astype(BF16)

            part = pl.ds(c * step * 2 * SEG, step * 2 * SEG)
            remote(far.at[part], near.at[part], far_send.at[c], far_recv.at[c], place.sibling).start()

        mine_a = sink_a.at[2 * place.pair_core + place.core]
        mine_a[...] = jnp.broadcast_to(jnp.sum(sink_sum[...], axis=1, keepdims=True), (1, BLOCK))
        for t, peer in enumerate((place.sibling, *place.twins)):
            remote(mine_a, mine_a, a_send, a_recv, peer).start()

        def collect(c):
            part = pl.ds(c * step * 2 * SEG, step * 2 * SEG)
            remote(far.at[part], near.at[part], far_send.at[c], far_recv.at[c], place.sibling).wait()

            @pl.loop(0, step)
            def _(i):
                n = c * step + i
                j = taken(head_of, n)
                for b in range(2):
                    last = entries[2, 2 * segment(place.half, j) + b]
                    at = n * (2 * SEG) + b * BLOCK
                    own = rows_of(n * SEG + b * BLOCK, BLOCK)
                    tk = (own_k[own, :] + term_k[last]) * SCALE + near[rows_of(at, BLOCK), :].astype(F32)
                    tv = own_v[own, :] + term_v[last] + near[rows_of(at + SEG, BLOCK), :].astype(F32)
                    fin[rows_of(at, BLOCK), :] = tk.astype(BF16)
                    fin[rows_of(at + SEG, BLOCK), :] = tv.astype(BF16)
                at = n * (2 * SEG)
                to = place.owner(j)
                by_relay, relay = place.relayed(j)
                slot = (head_of - place.row_head) * 4 + div(j, 4)

                @pl.when(by_relay)
                def _():
                    both = relay_kv.at[rows_of(slot * (2 * SEG), 2 * SEG)]
                    remote(fin.at[rows_of(at, 2 * SEG)], both, fin_send, relay_kv_recv.at[slot], relay).start()

                @pl.when(jnp.logical_not(by_relay))
                def _():
                    remote(fin.at[rows_of(at, SEG)], gk.at[0, :, cols], fin_send, out_recv.at[1], to).start()
                    remote(fin.at[rows_of(at + SEG, SEG)], gv.at[0, :, cols], fin_send, out_recv.at[2], to).start()

        collect(0)
        three = sink_a.at[pl.ds(0, 3)]
        remote(three, three, a_send, a_recv, place.sibling).wait()
        plane = div(place.plane, 2)
        mine_b = sink_b.at[plane]
        mine_b[...] = (sink_a[0] + sink_a[1]) + (sink_a[2] + sink_a[3])

        @pl.loop(1, PLANES)
        def _(i):
            remote(mine_b, mine_b, b_send, b_recv, place.other_plane(i)).start()

        collect(1)
        collect(2)
        seven = sink_b.at[pl.ds(0, PLANES - 1)]
        remote(seven, seven, b_send, b_recv, place.sibling).wait()
        total = sink_b[0]
        for i in range(1, PLANES):
            total = total + sink_b[i]
        sink_c[...] = total

        @pl.loop(0, HALF)
        def _(j):
            remote(sink_c, sink_out.at[head_of], c_send, c_recv, place.owner(j)).start()

        collect(3)
        remote(fin, fin, fin_send, out_recv.at[0], place.sibling).wait_send()
        remote(dq, dq, dq_send, out_recv.at[0], place.sibling).wait_send()

        @pl.loop(0, HALF)
        def _(j):
            remote(sink_c, sink_out.at[head_of], c_send, c_recv, place.owner(j)).wait_send()

    @pl.when(jnp.logical_not(place.is_home))
    def _():
        def each(work):
            @pl.loop(0, 4)
            def _(t):
                @pl.loop(0, place.homes)
                def _(i):
                    head, _ = place.row_home(i)
                    first = div(8 * head, 5) + HALF
                    j = rem(first - rem(first - place.x, 4) + HALF - 4 * div(t, 2) - 8 * rem(t, 2), HALF)

                    s = segment(place.half, j)

                    @pl.when(div(s, 4) != place.y)
                    def _():
                        work(i * 4 + div(j, 4), columns(head), (place.plane + place.row_core, s))

        def pass_dq(slot, cols, to):
            part = relay_dq.at[rows_of(slot * SEG, SEG)]
            remote(part, part, relay_send, relay_dq_recv.at[slot], place.sibling).wait_recv()
            remote(part, gq.at[0, :, cols], relay_send, out_recv.at[0], to).start()

        def pass_kv(slot, cols, to):
            at = slot * (2 * SEG)
            both = relay_kv.at[rows_of(at, 2 * SEG)]
            remote(both, both, relay_send, relay_kv_recv.at[slot], place.sibling).wait_recv()
            remote(relay_kv.at[rows_of(at, SEG)], gk.at[0, :, cols], relay_send, out_recv.at[1], to).start()
            remote(relay_kv.at[rows_of(at + SEG, SEG)], gv.at[0, :, cols], relay_send, out_recv.at[2], to).start()

        each(pass_dq)
        each(pass_kv)

        @pl.loop(0, 3 * place.homes * (4 - place.inside))
        def _(i):
            part = relay_dq.at[pl.ds(0, SEG)]
            remote(part, part, relay_send, relay_dq_recv.at[0], place.sibling).wait_send()

    remote(lists_in, lists_in, list_send, list_recv, place.sibling).wait_send()
    for t, ref in enumerate((q_in, g_in)):
        remote(ref, ref, qg_send.at[t], qg_recv.at[0], place.sibling).wait_send()
    for t, ref in enumerate((gq, gk, gv)):
        remote(ref, ref, dq_send, out_recv.at[t], place.sibling).wait_recv()
    remote(sink_out, sink_out, c_send, c_recv, place.sibling).wait_recv()


def settle_kernel(gq, gk, gv, out_q, out_k, out_v):
    out_q[...] = gq[...]
    out_k[...] = gk[...]
    out_v[...] = gv[...]


def body(query_in, key_in, value_in, grad_out, key_blocks, sink_logits):
    any_spec = pl.BlockSpec(memory_space=pl.ANY)
    smem_spec = pl.BlockSpec(memory_space=pltpu.SMEM)
    dma = pltpu.SemaphoreType.DMA
    shape = jax.ShapeDtypeStruct
    vmem = pltpu.VMEM
    local = local_of(lax.axis_index("ctx"))
    turns = turn(jnp.arange(HEADS, dtype=jnp.int32), local)
    lane = jnp.arange(BLOCK, dtype=jnp.int32)
    tiled = jnp.tile(jnp.pad(key_blocks[:, 0, :] + 1, ((0, 0), (0, SLOT - LISTED))), (1, HALF))
    lists = jnp.where(div(lane, SLOT)[None, :] == turns[:, None], tiled, 0)[:, None, :]
    tok = query_in.shape
    halves = (2, BLOCK, tok[2])
    gq, gk, gv, sink_rows = pl.pallas_call(
        fused_kernel,
        out_shape=(shape(tok, BF16), shape(tok, BF16), shape(tok, BF16), shape((HEADS, 1, BLOCK), F32)),
        in_specs=[any_spec] * 5 + [smem_spec],
        out_specs=(any_spec,) * 4,
        scratch_shapes=[
            vmem((NSEG * 4, BLOCK, HD), BF16),
            vmem((HALF * 2 * SEG, HD), BF16),
            vmem((HALF, 1, BLOCK), jnp.int32),
            vmem((8, BLOCK), jnp.int32),
            pltpu.SMEM((8, BLOCK), jnp.int32),
            vmem((HALF * SEG, HD), BF16),
            vmem((HALF * SLOT, BLOCK, HD), F32),
            vmem((HALF * SLOT, BLOCK, HD), F32),
            vmem((HALF * SEG, HD), F32),
            vmem((HALF * SEG, HD), F32),
            vmem((HALF * 2 * SEG, HD), BF16),
            vmem((HALF * 2 * SEG, HD), BF16),
            vmem((HALF * 2 * SEG, HD), BF16),
            vmem((KEYS, SEG), F32),
            vmem((KEYS, SEG), F32),
            vmem((1, SEG), F32),
            vmem((4, 1, BLOCK), F32),
            vmem((PLANES, 1, BLOCK), F32),
            vmem((1, BLOCK), F32),
            dma, dma, dma((2,)), dma((HALF,)), dma, dma, dma((2,)), dma((HALF,)), dma, dma,
            vmem((3 * 4 * SEG, HD), BF16), vmem((3 * 4 * 2 * SEG, HD), BF16),
            dma((12,)), dma((12,)), dma,
            dma((3,)), dma((CHUNKS,)), dma((CHUNKS,)), dma, dma, dma, dma, dma, dma, dma,
        ],
        compiler_params=pltpu.CompilerParams(
            collective_id=0, has_side_effects=True, vmem_limit_bytes=56 * 2**20
        ),
        name="fused",
    )(query_in, key_in.reshape(halves), value_in.reshape(halves), grad_out, lists, sink_logits)
    out = pl.pallas_call(
        settle_kernel,
        out_shape=(shape(tok, BF16),) * 3,
        in_specs=[pl.BlockSpec(memory_space=vmem)] * 3,
        out_specs=(pl.BlockSpec(memory_space=vmem),) * 3,
        name="settle",
    )(gq, gk, gv)
    return (*out, sink_rows[:, 0, 0])


def solution(mesh):
    placed = (
        P("dp", "ctx", None),
        P("dp", "ctx", None),
        P("dp", "ctx", None),
        P("dp", "ctx", None),
        P(None, "ctx", None),
        P(),
    )
    return jax.shard_map(
        body,
        mesh=mesh,
        in_specs=placed,
        out_specs=(P("dp", "ctx", None), P("dp", "ctx", None), P("dp", "ctx", None), P()),
        check_vma=False,
    )
```

```python
import math

import jax
import jax.numpy as jnp
from jax import lax
from jax.experimental import pallas as pl
from jax.experimental.pallas import tpu as pltpu
from jax.sharding import PartitionSpec as P

BLOCK = 128
SEG = 256
HD = 128
HEADS = 10
NSEG = 32
HALF = NSEG // 2
LISTED = 6
KEYS = SEG + LISTED * BLOCK
SLOT = 8
EMPTY = 6
CHUNKS = 4
EARLY = 0
PIECES = 4
PIECE = SEG // PIECES
PLANES = 8
LOG2E = math.log2(math.e)
SCALE = 1.0 / math.sqrt(HD)
MESH = pl.DeviceIdType.MESH
F32 = jnp.float32
BF16 = jnp.bfloat16
NT = (((1,), (1,)), ((), ()))
TN = (((0,), (0,)), ((), ()))


def div(a, b):
    return lax.div(a, jnp.int32(b))


def rem(a, b):
    return lax.rem(a, jnp.int32(b))


def home_ctx(core, head):
    j = 2 * div(head, 5) + core
    r = rem(head, 5)
    odd = div(r, 3)
    x = rem(r + j + 8 + odd * (r - 6), 4)
    return 4 * (2 * j + odd) + x


def my_pair(ctx):
    y = div(ctx, 4)
    j = div(y, 2)
    odd = rem(y, 2)
    u = rem(rem(ctx, 4) + 4 - j, 4)
    is_home = ((1 - odd) * div(u, 3) + odd * rem(u, 2)) == 0
    r = (1 - odd) * u + odd * (3 + div(u, 2))
    return is_home, rem(j, 2), 5 * div(j, 2) + r


def half_of(s):
    return rem(div(s, 8), 2)


def local_of(s):
    return 8 * div(s, HALF) + rem(s, 8)


def segment(half, j):
    return HALF * div(j, 8) + 8 * half + rem(j, 8)


def is_spare(y, x):
    u = rem(x + 4 - div(y, 2), 4)
    odd = rem(y, 2)
    return ((1 - odd) * div(u, 3) + odd * rem(u, 2)) == 1


def turn(head, j):
    m = rem(div(8 * head, 5) + HALF - j, HALF)
    return 2 * rem(m, HALF // 2) + div(m, HALF // 2)


def taken(head, n):
    m = div(n, 2) + (HALF // 2) * rem(n, 2)
    return rem(div(8 * head, 5) + HALF - m, HALF)


class Place:
    def __init__(self):
        dp = lax.axis_index("dp")
        self.ctx = lax.axis_index("ctx")
        self.core = rem(dp, 2)
        self.plane = dp - self.core
        self.is_home, self.pair_core, self.pair_head = my_pair(self.ctx)
        self.target_core = 1 - half_of(self.ctx)
        self.half = 1 - self.core
        self.local = local_of(self.ctx)
        self.first = rem(div(5 * self.local + 7, 8), HEADS)
        self.sibling = (self.plane + 1 - self.core, self.ctx)
        self.y = div(self.ctx, 4)
        self.x = rem(self.ctx, 4)
        self.odd = rem(self.y, 2)
        self.spares = 1 + self.odd
        self.homes = 3 - self.odd
        self.row_head = 5 * div(self.y, 4) + 3 * self.odd
        self.row_core = rem(div(self.y, 2), 2)
        self.inside = (self.row_core == self.half).astype(jnp.int32)
        twin = home_ctx(1 - self.pair_core, self.pair_head)
        self.twins = ((self.plane, twin), (self.plane + 1, twin))

    def home(self, head):
        return (self.plane + self.target_core, home_ctx(self.core, head))

    def sent_to(self, i):
        return rem(self.first + div(i, 2) + (HEADS // 2) * rem(i, 2), HEADS)

    def owner(self, j):
        return (self.plane + self.pair_core, segment(self.half, j))

    def row_home(self, i):
        head = self.row_head + i
        return head, (self.plane + self.core, home_ctx(self.row_core, head))

    def relayed(self, j):
        x = rem(j, 4)
        device = (self.plane + self.core, 4 * self.y + x)
        outer = (self.odd == 1) | (self.pair_head != self.row_head + 1)
        return is_spare(self.y, x) & (div(segment(self.half, j), 4) != self.y) & outer, device

    def other_plane(self, i):
        return (rem(self.plane + self.core + 2 * i, 2 * PLANES), self.ctx)


def greet(place):
    barrier = pltpu.get_barrier_semaphore()

    def signal(device):
        pl.semaphore_signal(barrier, inc=1, device_id=device, device_id_type=MESH)

    @pl.loop(0, HEADS)
    def _(i):
        signal(place.home(i))

    @pl.loop(0, 4)
    def _(i):
        y = 4 * div(i, 2) + 2 * place.core + rem(i, 2)

        @pl.when(is_spare(y, place.x) & (y != place.y))
        def _():
            signal((place.plane + place.target_core, 4 * y + place.x))

    @pl.when(jnp.logical_not(place.is_home))
    def _():
        @pl.loop(0, place.homes)
        def _(i):
            signal(place.row_home(i)[1])

    @pl.when(place.is_home)
    def _():
        @pl.loop(0, HALF)
        def _(j):
            signal(place.owner(j))

        signal(place.sibling)
        for twin in place.twins:
            signal(twin)

        @pl.loop(1, PLANES)
        def _(i):
            signal(place.other_plane(i))

    home = place.is_home.astype(jnp.int32)
    peers = HALF + 1 + 2 + PLANES - 1 + place.spares
    pl.semaphore_wait(barrier, HEADS + home * peers + (1 - home) * (4 - place.inside))


def remote(src, dst, ssem, rsem, target):
    return pltpu.make_async_remote_copy(
        src_ref=src, dst_ref=dst, send_sem=ssem, recv_sem=rsem,
        device_id=target, device_id_type=MESH,
    )


def columns(head):
    return pl.ds(pl.multiple_of(head * HD, HD), HD)


def rows_of(start, size):
    return pl.ds(pl.multiple_of(start, size), size)


def fold(x, op):
    return op(x.reshape(x.shape[0] // 8, 8, x.shape[1]), axis=0)


def highest(x):
    part = x[0:8]
    for i in range(8, x.shape[0], 8):
        part = jnp.maximum(part, x[i:i + 8])
    row = part[0:1]
    for i in range(1, 8):
        row = jnp.maximum(row, part[i:i + 1])
    return row


def write_tables(lists, table):
    row = lists[0]
    for j in range(1, HALF):
        row = row + lists[j]
    row = row - 1
    shape = (BLOCK, BLOCK)
    wide = jnp.broadcast_to(row, shape)
    tall = wide.T
    entry = lax.broadcasted_iota(jnp.int32, shape, 0)
    lane = lax.broadcasted_iota(jnp.int32, shape, 1)
    before = highest(jnp.where((tall == wide) & (entry < lane), entry, -1))
    last = highest(jnp.where(tall == lane, entry, -1))
    place = jnp.maximum(row, 0)
    block = lax.bitwise_and(place, 1)
    s = lax.shift_right_logical(place, 1)
    half = lax.bitwise_and(lax.shift_right_logical(s, 3), 1)
    local = 8 * lax.shift_right_logical(s, 4) + lax.bitwise_and(s, 7)
    table[0:1, :] = 4 * (half * HALF + local) + block
    table[1:2, :] = jnp.where(before < 0, EMPTY, before)
    table[2:3, :] = jnp.where(last < 0, EMPTY, last)


def fused_kernel(
    q_in, k_in, v_in, g_in, lists_in, sinks, gq, gk, gv, sink_out,
    kv, qg, lists, table, entries, dq, term_k, term_v, own_k, own_v, far, near, fin, e_ref, p_ref,
    sink_sum, sink_a, sink_b, sink_c,
    list_send, list_recv, kv_send, kv_recv, swap_send, swap_recv, qg_send, qg_recv, dq_send, fin_send,
    relay_dq, relay_kv, relay_dq_recv, relay_kv_recv, relay_send,
    out_recv, far_send, far_recv, a_send, a_recv, b_send, b_recv, c_send, c_recv, table_sem,
):
    place = Place()
    greet(place)
    head_of = place.pair_head

    @pl.loop(0, HEADS)
    def _(i):
        head = place.sent_to(i)
        target = place.home(head)
        remote(lists_in.at[head], lists.at[place.local], list_send, list_recv, target).start()

    for block in range(2):
        for p in range(PIECES // 2):
            rows = pl.ds(p * PIECE, PIECE)

            @pl.loop(0, HEADS)
            def _(i):
                head = place.sent_to(i)
                cols = columns(head)
                target = place.home(head)
                at = 4 * ((1 - place.target_core) * HALF + place.local) + block
                sem = kv_recv.at[place.local]
                remote(k_in.at[block, rows, cols], kv.at[at, rows], kv_send.at[0], sem, target).start()
                remote(v_in.at[block, rows, cols], kv.at[at + 2, rows], kv_send.at[1], sem, target).start()

    def pass_on(start, stop):
        @pl.loop(start, stop)
        def _(n):
            j = taken(head_of, n)
            part = kv.at[pl.ds(4 * (place.half * HALF + j), 4)]
            remote(part, part, kv_send.at[0], kv_recv.at[j], place.sibling).wait_recv()
            remote(part, part, swap_send, swap_recv, place.sibling).start()

    @pl.when(place.is_home)
    def _():
        remote(lists, lists, list_send, list_recv, place.sibling).wait_recv()
        write_tables(lists, table)
        down = pltpu.make_async_copy(table, entries, table_sem)
        down.start()
        term_k[EMPTY] = jnp.zeros((BLOCK, HD), F32)
        term_v[EMPTY] = jnp.zeros((BLOCK, HD), F32)
        sink_sum[...] = jnp.zeros_like(sink_sum)
        down.wait()

        pass_on(0, EARLY)

    for t, ref in enumerate((k_in, v_in)):
        remote(ref, ref, kv_send.at[t], kv_recv.at[0], place.sibling).wait_send()

    @pl.loop(0, HEADS)
    def _(i):
        head = place.sent_to(i)
        cols = columns(head)
        target = place.home(head)
        at = place.local * (2 * SEG)
        sem = qg_recv.at[place.local]
        remote(q_in.at[0, :, cols], qg.at[rows_of(at, SEG)], qg_send.at[0], sem, target).start()
        remote(g_in.at[0, :, cols], qg.at[rows_of(at + SEG, SEG)], qg_send.at[1], sem, target).start()

    @pl.when(place.is_home)
    def _():
        cols = columns(head_of)
        pass_on(EARLY, HALF)
        mine = kv.at[pl.ds(place.half * (4 * HALF), 4 * HALF)]
        other = kv.at[pl.ds(place.core * (4 * HALF), 4 * HALF)]
        remote(mine, other, swap_send, swap_recv, place.sibling).wait()
        sink2 = sinks[head_of] * LOG2E

        @pl.loop(0, HALF)
        def _(n):
            j = taken(head_of, n)
            part = qg.at[rows_of(j * (2 * SEG), 2 * SEG)]
            remote(part, part, qg_send.at[0], qg_recv.at[j], place.sibling).wait_recv()
            q = qg[rows_of(j * (2 * SEG), SEG), :]
            g = qg[rows_of(j * (2 * SEG) + SEG, SEG), :]
            spans = [(4 * (place.half * HALF + j), 0, SEG)]
            for m in range(LISTED):
                spans.append((entries[0, n * SLOT + m], SEG + m * BLOCK, BLOCK))

            def keyed(src, size):
                return kv[pl.ds(src, 2)].reshape(SEG, HD) if size == SEG else kv[src]

            top8 = None
            for src, at, size in spans:
                k = keyed(src, size)
                s = lax.dot_general(k, q, NT, preferred_element_type=F32)
                e_ref[at:at + size, :] = s
                high = fold(s, jnp.max)
                top8 = high if top8 is None else jnp.maximum(top8, high)
            factor = SCALE * LOG2E
            top = jnp.maximum(jnp.max(top8, axis=0, keepdims=True) * factor, sink2)
            sum8 = jnp.zeros((8, SEG), F32)
            dot8 = jnp.zeros((8, SEG), F32)
            for src, at, size in spans:
                v = keyed(src + 2, size)
                dp = lax.dot_general(v, g, NT, preferred_element_type=F32)
                e = jnp.exp2(e_ref[at:at + size, :] * factor - top)
                e_ref[at:at + size, :] = e
                p_ref[at:at + size, :] = dp
                sum8 = sum8 + fold(e, jnp.sum)
                dot8 = dot8 + fold(e * dp, jnp.sum)
            sink_e = jnp.exp2(sink2 - top)
            total = sink_e + jnp.sum(sum8, axis=0, keepdims=True)
            inv = 1.0 / total
            delta = jnp.sum(dot8, axis=0, keepdims=True) * inv
            sink_sum[...] = sink_sum[...] - sink_e * inv * delta
            dq_t = jnp.zeros((HD, SEG), F32)
            for m, (src, at, size) in enumerate(spans):
                w = e_ref[at:at + size, :] * inv
                ds = (w * (p_ref[at:at + size, :] - delta)).astype(BF16)
                w = w.astype(BF16)
                tv = jnp.dot(w, g, preferred_element_type=F32)
                tk = jnp.dot(ds, q, preferred_element_type=F32)
                if m == 0:
                    own_k[rows_of(n * SEG, SEG), :] = tk
                    own_v[rows_of(n * SEG, SEG), :] = tv
                else:
                    slot = n * SLOT + m - 1
                    before = entries[1, slot]
                    term_k[slot] = tk + term_k[before]
                    term_v[slot] = tv + term_v[before]
                k = keyed(src, size)
                dq_t = dq_t + lax.dot_general(k, ds, TN, preferred_element_type=F32)
            rows = rows_of(n * SEG, SEG)
            dq[rows, :] = (dq_t * SCALE).T.astype(BF16)
            by_relay, relay = place.relayed(j)
            slot = (head_of - place.row_head) * 4 + div(j, 4)

            @pl.when(by_relay)
            def _():
                to = relay_dq.at[rows_of(slot * SEG, SEG)]
                remote(dq.at[rows], to, dq_send, relay_dq_recv.at[slot], relay).start()

            @pl.when(jnp.logical_not(by_relay))
            def _():
                remote(dq.at[rows], gq.at[0, :, cols], dq_send, out_recv.at[0], place.owner(j)).start()

        step = HALF // CHUNKS
        for c in range(CHUNKS):
            @pl.loop(0, step)
            def _(i):
                n = c * step + i
                j = taken(head_of, n)
                for b in range(2):
                    last = entries[2, 2 * segment(place.core, j) + b]
                    at = n * (2 * SEG) + b * BLOCK
                    far[rows_of(at, BLOCK), :] = (term_k[last] * SCALE).astype(BF16)
                    far[rows_of(at + SEG, BLOCK), :] = term_v[last].astype(BF16)

            part = pl.ds(c * step * 2 * SEG, step * 2 * SEG)
            remote(far.at[part], near.at[part], far_send.at[c], far_recv.at[c], place.sibling).start()

        mine_a = sink_a.at[2 * place.pair_core + place.core]
        mine_a[...] = jnp.broadcast_to(jnp.sum(sink_sum[...], axis=1, keepdims=True), (1, BLOCK))
        for t, peer in enumerate((place.sibling, *place.twins)):
            remote(mine_a, mine_a, a_send, a_recv, peer).start()

        def collect(c):
            part = pl.ds(c * step * 2 * SEG, step * 2 * SEG)
            remote(far.at[part], near.at[part], far_send.at[c], far_recv.at[c], place.sibling).wait()

            @pl.loop(0, step)
            def _(i):
                n = c * step + i
                j = taken(head_of, n)
                for b in range(2):
                    last = entries[2, 2 * segment(place.half, j) + b]
                    at = n * (2 * SEG) + b * BLOCK
                    own = rows_of(n * SEG + b * BLOCK, BLOCK)
                    tk = (own_k[own, :] + term_k[last]) * SCALE + near[rows_of(at, BLOCK), :].astype(F32)
                    tv = own_v[own, :] + term_v[last] + near[rows_of(at + SEG, BLOCK), :].astype(F32)
                    fin[rows_of(at, BLOCK), :] = tk.astype(BF16)
                    fin[rows_of(at + SEG, BLOCK), :] = tv.astype(BF16)
                at = n * (2 * SEG)
                to = place.owner(j)
                by_relay, relay = place.relayed(j)
                slot = (head_of - place.row_head) * 4 + div(j, 4)

                @pl.when(by_relay)
                def _():
                    for t in range(2):
                        to = relay_kv.at[rows_of(slot * (2 * SEG) + t * SEG, SEG)]
                        sem = relay_kv_recv.at[2 * slot + t]
                        remote(fin.at[rows_of(at + t * SEG, SEG)], to, fin_send, sem, relay).start()

                @pl.when(jnp.logical_not(by_relay))
                def _():
                    remote(fin.at[rows_of(at, SEG)], gk.at[0, :, cols], fin_send, out_recv.at[1], to).start()
                    remote(fin.at[rows_of(at + SEG, SEG)], gv.at[0, :, cols], fin_send, out_recv.at[2], to).start()

        collect(0)
        three = sink_a.at[pl.ds(0, 3)]
        remote(three, three, a_send, a_recv, place.sibling).wait()
        plane = div(place.plane, 2)
        mine_b = sink_b.at[plane]
        mine_b[...] = (sink_a[0] + sink_a[1]) + (sink_a[2] + sink_a[3])

        @pl.loop(1, PLANES)
        def _(i):
            remote(mine_b, mine_b, b_send, b_recv, place.other_plane(i)).start()

        collect(1)
        collect(2)
        seven = sink_b.at[pl.ds(0, PLANES - 1)]
        remote(seven, seven, b_send, b_recv, place.sibling).wait()
        total = sink_b[0]
        for i in range(1, PLANES):
            total = total + sink_b[i]
        sink_c[...] = total

        @pl.loop(0, HALF)
        def _(j):
            remote(sink_c, sink_out.at[head_of], c_send, c_recv, place.owner(j)).start()

        collect(3)
        remote(fin, fin, fin_send, out_recv.at[0], place.sibling).wait_send()
        remote(dq, dq, dq_send, out_recv.at[0], place.sibling).wait_send()

        @pl.loop(0, HALF)
        def _(j):
            remote(sink_c, sink_out.at[head_of], c_send, c_recv, place.owner(j)).wait_send()

    @pl.when(jnp.logical_not(place.is_home))
    def _():
        def each(work):
            @pl.loop(0, 4)
            def _(t):
                @pl.loop(0, place.homes)
                def _(i):
                    head, _ = place.row_home(i)
                    first = div(8 * head, 5) + HALF
                    j = rem(first - rem(first - place.x, 4) + HALF - 4 * div(t, 2) - 8 * rem(t, 2), HALF)

                    s = segment(place.half, j)

                    @pl.when((div(s, 4) != place.y) & ((place.odd == 1) | (i != 1)))
                    def _():
                        work(i * 4 + div(j, 4), columns(head), (place.plane + place.row_core, s))

        def pass_dq(slot, cols, to):
            part = relay_dq.at[rows_of(slot * SEG, SEG)]
            remote(part, part, relay_send, relay_dq_recv.at[slot], place.sibling).wait_recv()
            remote(part, gq.at[0, :, cols], relay_send, out_recv.at[0], to).start()

        def pass_kv(slot, cols, to):
            for t, ref in enumerate((gk, gv)):
                part = relay_kv.at[rows_of(slot * (2 * SEG) + t * SEG, SEG)]
                remote(part, part, relay_send, relay_kv_recv.at[2 * slot + t], place.sibling).wait_recv()
                remote(part, ref.at[0, :, cols], relay_send, out_recv.at[1 + t], to).start()

        each(pass_dq)
        each(pass_kv)

        @pl.loop(0, 3 * 2 * (4 - place.inside))
        def _(i):
            part = relay_dq.at[pl.ds(0, SEG)]
            remote(part, part, relay_send, relay_dq_recv.at[0], place.sibling).wait_send()

    remote(lists_in, lists_in, list_send, list_recv, place.sibling).wait_send()
    for t, ref in enumerate((q_in, g_in)):
        remote(ref, ref, qg_send.at[t], qg_recv.at[0], place.sibling).wait_send()
    for t, ref in enumerate((gq, gk, gv)):
        remote(ref, ref, dq_send, out_recv.at[t], place.sibling).wait_recv()
    remote(sink_out, sink_out, c_send, c_recv, place.sibling).wait_recv()


def settle_kernel(gq, gk, gv, sink_rows, out_q, out_k, out_v, out_sink):
    for head in range(HEADS):
        out_sink[head] = sink_rows[head, 0, 0]
    out_q[...] = gq[...]
    out_k[...] = gk[...]
    out_v[...] = gv[...]


def body(query_in, key_in, value_in, grad_out, key_blocks, sink_logits):
    any_spec = pl.BlockSpec(memory_space=pl.ANY)
    smem_spec = pl.BlockSpec(memory_space=pltpu.SMEM)
    dma = pltpu.SemaphoreType.DMA
    shape = jax.ShapeDtypeStruct
    vmem = pltpu.VMEM
    local = local_of(lax.axis_index("ctx"))
    turns = turn(jnp.arange(HEADS, dtype=jnp.int32), local)
    lane = jnp.arange(BLOCK, dtype=jnp.int32)
    tiled = jnp.tile(jnp.pad(key_blocks[:, 0, :] + 1, ((0, 0), (0, SLOT - LISTED))), (1, HALF))
    lists = jnp.where(div(lane, SLOT)[None, :] == turns[:, None], tiled, 0)[:, None, :]
    tok = query_in.shape
    halves = (2, BLOCK, tok[2])
    gq, gk, gv, sink_rows = pl.pallas_call(
        fused_kernel,
        out_shape=(shape(tok, BF16), shape(tok, BF16), shape(tok, BF16), shape((HEADS, 1, BLOCK), F32)),
        in_specs=[any_spec] * 5 + [smem_spec],
        out_specs=(any_spec,) * 4,
        scratch_shapes=[
            vmem((NSEG * 4, BLOCK, HD), BF16),
            vmem((HALF * 2 * SEG, HD), BF16),
            vmem((HALF, 1, BLOCK), jnp.int32),
            vmem((8, BLOCK), jnp.int32),
            pltpu.SMEM((8, BLOCK), jnp.int32),
            vmem((HALF * SEG, HD), BF16),
            vmem((HALF * SLOT, BLOCK, HD), F32),
            vmem((HALF * SLOT, BLOCK, HD), F32),
            vmem((HALF * SEG, HD), F32),
            vmem((HALF * SEG, HD), F32),
            vmem((HALF * 2 * SEG, HD), BF16),
            vmem((HALF * 2 * SEG, HD), BF16),
            vmem((HALF * 2 * SEG, HD), BF16),
            vmem((KEYS, SEG), F32),
            vmem((KEYS, SEG), F32),
            vmem((1, SEG), F32),
            vmem((4, 1, BLOCK), F32),
            vmem((PLANES, 1, BLOCK), F32),
            vmem((1, BLOCK), F32),
            dma, dma, dma((2,)), dma((HALF,)), dma, dma, dma((2,)), dma((HALF,)), dma, dma,
            vmem((3 * 4 * SEG, HD), BF16), vmem((3 * 4 * 2 * SEG, HD), BF16),
            dma((12,)), dma((24,)), dma,
            dma((3,)), dma((CHUNKS,)), dma((CHUNKS,)), dma, dma, dma, dma, dma, dma, dma,
        ],
        compiler_params=pltpu.CompilerParams(
            collective_id=0, has_side_effects=True, vmem_limit_bytes=56 * 2**20
        ),
        name="fused",
    )(query_in, key_in.reshape(halves), value_in.reshape(halves), grad_out, lists, sink_logits)
    out = pl.pallas_call(
        settle_kernel,
        out_shape=(shape(tok, BF16), shape(tok, BF16), shape(tok, BF16), shape((HEADS,), F32)),
        in_specs=[pl.BlockSpec(memory_space=vmem)] * 3 + [smem_spec],
        out_specs=(*(pl.BlockSpec(memory_space=vmem),) * 3, smem_spec),
        name="settle",
    )(gq, gk, gv, sink_rows)
    return out


def solution(mesh):
    placed = (
        P("dp", "ctx", None),
        P("dp", "ctx", None),
        P("dp", "ctx", None),
        P("dp", "ctx", None),
        P(None, "ctx", None),
        P(),
    )
    return jax.shard_map(
        body,
        mesh=mesh,
        in_specs=placed,
        out_specs=(P("dp", "ctx", None), P("dp", "ctx", None), P("dp", "ctx", None), P()),
        check_vma=False,
    )
```
